32 devices in a mesh: dp: 8 (over z, x), mp: 4 (over y, core).
Axes of the slice: x: 2, y: 2, z: 4, core: 2. Of those that a mesh axis runs over, the one named last changes fastest.
Arguments:
- text_blocks: bfloat16 [256, 64, 768], P(('dp', 'mp')), may hold values from -6 to 6
- visual_blocks: bfloat16 [256, 40, 768], P(('dp', 'mp')), may hold values from -6 to 6
- drop_flags: int32 [256, 2], P('dp'), may hold values 0 or 1
- qkv_weight: bfloat16 [4, 768, 3, 768], P(None, None, None, 'mp'), may hold values from -0.21875 to 0.21875
- out_weight: bfloat16 [4, 768, 768], P(None, 'mp'), may hold values from -0.625 to 0.625
- up_weight: bfloat16 [2, 768, 3072], P(None, None, 'mp'), may hold values from -0.21875 to 0.21875
- down_weight: bfloat16 [2, 3072, 768], P(None, 'mp'), may hold values from -0.109375 to 0.109375
- norm_gain: float32 [6, 768], replicated, may hold values from 0.5 to 1.5
- norm_shift: float32 [6, 768], replicated, may hold values from -3 to 3
- text_cotangent: bfloat16 [256, 64, 768], P(('dp', 'mp')), may hold values from -6 to 6
- visual_cotangent: bfloat16 [256, 40, 768], P(('dp', 'mp')), may hold values from -6 to 6
Outputs:
- text_output: bfloat16 [256, 64, 768], P(('dp', 'mp'))
- visual_output: bfloat16 [256, 40, 768], P(('dp', 'mp'))
- text_gradient: bfloat16 [256, 64, 768], P(('dp', 'mp'))
- visual_gradient: bfloat16 [256, 40, 768], P(('dp', 'mp'))
- qkv_gradient: float32 [4, 768, 3, 768], P(None, None, None, 'mp')
- out_gradient: float32 [4, 768, 768], P(None, 'mp')
- up_gradient: float32 [2, 768, 3072], P(None, None, 'mp')
- down_gradient: float32 [2, 3072, 768], P(None, 'mp')
- gain_gradient: float32 [6, 768], replicated
- shift_gradient: float32 [6, 768], replicated
The draws below stay inside these ranges and needn't reach their ends.
Inputs may be any that keep to these rules, and one draw needn't show every extreme that they name: drop_flags[:, 0] = 1 marks a page whose text is absent, drop_flags[:, 1] = 1 one whose visual blocks are absent.
All inputs are finite; a program needn't handle non-finite values.
Results may differ from the reference program's by a relative error of at most 0.025.
Values may be sent and summed in bfloat16 or wider, within the bound.
No kernel may reach another device: no remote copies, remote signals or barrier semaphores. Data moves between devices by JAX's collectives and lax.ppermute only.
A program may use at most 256 MiB of HBM per device.

```python
import jax
import jax.numpy as jnp
from jax import lax

D = 768
HEADS = 12
HEAD = 64
FF = 3072
TLEN = 64
VLEN = 40
PAGES = 256


def with_ends(values, stream_key, least, largest):
    spot = [jax.random.randint(jax.random.fold_in(stream_key, axis), (), 0, length) for axis, length in enumerate(values.shape)]
    main_axis = values.shape.index(max(values.shape))
    next_to = spot[:main_axis] + [(spot[main_axis] + 1) % values.shape[main_axis]] + spot[main_axis + 1:]
    return values.at[tuple(spot)].set(least).at[tuple(next_to)].set(largest)


def level_of(stream_key, extent, cuts, smallest, high):
    def one(dim, shards_of):
        heights = jax.random.uniform(jax.random.fold_in(jax.random.fold_in(stream_key, 6), dim), (shards_of,), jnp.float32, smallest / len(cuts), high / len(cuts))
        return jnp.repeat(jnp.exp(heights), extent[dim] // shards_of).reshape((-1,) + (1,) * (len(extent) - dim - 1))

    loudness = one(*cuts[0])
    for cut in cuts[1:]:
        loudness = loudness * one(*cut)
    return loudness


def bell_draw(stream_key, shape, deviation, bound, pieces=(), kind=jnp.bfloat16):
    entries = deviation * jax.random.normal(stream_key, shape, jnp.float32)
    if pieces:
        entries = entries * level_of(stream_key, shape, pieces, -0.22, 0.18)
    return jnp.clip(entries, -bound, bound).astype(kind)


def setup_inputs(seed: int = 0) -> dict:
    key_of = jax.random.split(jax.random.key(seed), 12)
    text_blocks = bell_draw(key_of[0], (PAGES, TLEN, D), 1.0, 6.0, ((0, 32),))
    visual_blocks = bell_draw(key_of[1], (PAGES, VLEN, D), 1.0, 6.0, ((0, 32),))
    drop_flags = with_ends((jax.random.randint(key_of[2], (PAGES, 2), 0, 4) < 1).astype(jnp.int32), jax.random.fold_in(key_of[2], 1), 0, 1)
    qkv_weight = bell_draw(key_of[3], (4, D, 3, D), D ** -0.5, 0.21875, ((3, 4),))
    out_weight = bell_draw(key_of[4], (4, D, D), (D // 8) ** -0.5, 0.625, ((1, 4),))
    up_weight = bell_draw(key_of[5], (2, D, FF), D ** -0.5, 0.21875, ((2, 4),))
    down_weight = bell_draw(key_of[6], (2, FF, D), FF ** -0.5, 0.109375, ((1, 4),))
    norm_gain = jnp.clip(1.0 + 0.1 * jax.random.normal(key_of[7], (6, D), jnp.float32), 0.5, 1.5)
    norm_shift = bell_draw(key_of[8], (6, D), 0.5, 3.0, (), jnp.float32)
    text_cotangent = bell_draw(key_of[9], (PAGES, TLEN, D), 1.0, 6.0, ((0, 32),))
    visual_cotangent = bell_draw(key_of[10], (PAGES, VLEN, D), 1.0, 6.0, ((0, 32),))
    return {"text_blocks": text_blocks, "visual_blocks": visual_blocks, "drop_flags": drop_flags, "qkv_weight": qkv_weight, "out_weight": out_weight, "up_weight": up_weight, "down_weight": down_weight, "norm_gain": norm_gain, "norm_shift": norm_shift, "text_cotangent": text_cotangent, "visual_cotangent": visual_cotangent}


@jax.custom_vjp
def low(v):
    return lax.optimization_barrier(v.astype(jnp.bfloat16)).astype(jnp.float32)

@jax.custom_vjp
def low_back(v):
    return v

def low_keep(v):
    return (low(v), None)

def low_pass(kept, grad):
    return (grad,)

def back_keep(v):
    return (v, None)

def back_low(kept, grad):
    return (low(grad),)
low.defvjp(low_keep, low_pass)
low_back.defvjp(back_keep, back_low)
EPSILON = 1e-05
HIGHEST = lax.Precision.HIGHEST

def project(activation, weight):
    return jnp.einsum('pld,de->ple', activation, weight, precision=HIGHEST)

def split_heads(values):
    return values.reshape(values.shape[0], values.shape[1], HEADS, HEAD)

def layer_norm(values, gain, shift):
    center = values - lax.optimization_barrier(jnp.mean(values, axis=-1, keepdims=True))
    spread = lax.optimization_barrier(jnp.mean(center * center, axis=-1, keepdims=True))
    return center * lax.rsqrt(spread + EPSILON) * gain + shift

def attend(query_side, key_side, weight_block, out_block, keep_mask):
    queries = low_back(low(project(query_side, weight_block[:, 0])))
    key_block = low_back(low(project(key_side, weight_block[:, 1])))
    value_block = low_back(low(project(key_side, weight_block[:, 2])))
    raw = jnp.einsum('pqhe,pkhe->phqk', split_heads(queries), split_heads(key_block), precision=HIGHEST)
    scores = low_back(raw * HEAD ** (-0.5))
    probability = low(jax.nn.softmax(scores, axis=-1))
    context = jnp.einsum('phqk,pkhe->pqhe', probability, split_heads(value_block), precision=HIGHEST)
    context = context.reshape(query_side.shape[0], query_side.shape[1], HEADS * HEAD)
    if keep_mask is not None:
        context = context * keep_mask[:, None, None]
    context = low_back(low(context))
    return project(context, out_block)

def feed_forward(activation, up_block, down_block):
    before = low_back(project(activation, up_block))
    hidden = low(jax.nn.gelu(before))
    return project(hidden, down_block)

def forward(text_now, visual_now, qkv_weight, out_weight, up_weight, down_weight, norm_gain, norm_shift, keep_text, keep_visual):
    text_norm = low(layer_norm(text_now, norm_gain[0], norm_shift[0]))
    visual_norm = low(layer_norm(visual_now, norm_gain[1], norm_shift[1]))
    text_next = text_now + low_back(attend(text_norm, visual_norm, qkv_weight[0], out_weight[0], keep_visual))
    visual_next = visual_now + low_back(attend(visual_norm, text_norm, qkv_weight[1], out_weight[1], keep_text))
    text_norm = low(layer_norm(text_next, norm_gain[2], norm_shift[2]))
    visual_norm = low(layer_norm(visual_next, norm_gain[3], norm_shift[3]))
    text_after = text_next + low_back(attend(text_norm, text_norm, qkv_weight[2], out_weight[2], None))
    visual_after = visual_next + low_back(attend(visual_norm, visual_norm, qkv_weight[3], out_weight[3], None))
    text_norm = low(layer_norm(text_after, norm_gain[4], norm_shift[4]))
    visual_norm = low(layer_norm(visual_after, norm_gain[5], norm_shift[5]))
    text_final = text_after + low_back(feed_forward(text_norm, up_weight[0], down_weight[0]))
    visual_final = visual_after + low_back(feed_forward(visual_norm, up_weight[1], down_weight[1]))
    return (text_final, visual_final)

def reference(text_blocks, visual_blocks, drop_flags, qkv_weight, out_weight, up_weight, down_weight, norm_gain, norm_shift, text_cotangent, visual_cotangent):
    keep_text = (1 - drop_flags[:, 0]).astype(jnp.float32)
    keep_visual = (1 - drop_flags[:, 1]).astype(jnp.float32)

    def layer(text_now, visual_now, qkv_now, out_now, up_now, down_now, gain_now, shift_now):
        return forward(text_now, visual_now, qkv_now, out_now, up_now, down_now, gain_now, shift_now, keep_text, keep_visual)
    outputs, pullback = jax.vjp(layer, text_blocks.astype(jnp.float32), visual_blocks.astype(jnp.float32), qkv_weight.astype(jnp.float32), out_weight.astype(jnp.float32), up_weight.astype(jnp.float32), down_weight.astype(jnp.float32), norm_gain.astype(jnp.float32), norm_shift.astype(jnp.float32))
    gradients = pullback((text_cotangent.astype(jnp.float32), visual_cotangent.astype(jnp.float32)))
    return (outputs[0].astype(jnp.bfloat16), outputs[1].astype(jnp.bfloat16), gradients[0].astype(jnp.bfloat16), gradients[1].astype(jnp.bfloat16), gradients[2], gradients[3], gradients[4], gradients[5], gradients[6], gradients[7])
```

```python
import jax
import jax.numpy as jnp
from jax import lax
from jax.sharding import PartitionSpec as P

HEAD = 64


EPSILON = 1e-05


def normalize(values, gain, shift):
    center = values - jnp.mean(values, axis=-1, keepdims=True)
    spread = jnp.mean(center * center, axis=-1, keepdims=True)
    return center * lax.rsqrt(spread + EPSILON) * gain + shift


def linear(activation, weight):
    return jnp.einsum("pld,de->ple", activation, weight, preferred_element_type=jnp.float32)


def linear_back(gradient, weight):
    return jnp.einsum("ple,de->pld", gradient, weight, preferred_element_type=jnp.float32)


def weight_grad(activation, gradient):
    return jnp.einsum("pld,ple->de", activation, gradient, preferred_element_type=jnp.float32)


def split_heads(values):
    return values.reshape(values.shape[0], values.shape[1], values.shape[2] // HEAD, HEAD)


def merge_heads(values):
    return values.reshape(values.shape[0], values.shape[1], values.shape[2] * values.shape[3])


def score_block(queries, key_block):
    raw = jnp.einsum(
        "pqhe,pkhe->phqk",
        split_heads(queries),
        split_heads(key_block),
        preferred_element_type=jnp.float32,
    )
    return raw * HEAD ** (-0.5)


def attend_context(query_side, key_side, weight_block, keep_mask):
    queries = linear(query_side, weight_block[:, 0]).astype(jnp.bfloat16)
    key_block = linear(key_side, weight_block[:, 1]).astype(jnp.bfloat16)
    value_block = linear(key_side, weight_block[:, 2]).astype(jnp.bfloat16)
    scores = score_block(queries, key_block)
    row_max = jnp.max(scores, axis=-1, keepdims=True)
    log_total = row_max + jnp.log(jnp.sum(jnp.exp(scores - row_max), axis=-1, keepdims=True))
    probability = jnp.exp(scores - log_total).astype(jnp.bfloat16)
    context = merge_heads(
        jnp.einsum(
            "phqk,pkhe->pqhe",
            probability,
            split_heads(value_block),
            preferred_element_type=jnp.float32,
        )
    )
    if keep_mask is not None:
        context = context * keep_mask[:, None, None]
    context = context.astype(jnp.bfloat16)
    return (context, (queries, key_block, value_block, log_total, context))


def attend_back(query_side, key_side, weight_block, out_block, keep_mask, saved, out_grad):
    queries, key_block, value_block, log_total, context = saved
    out_weight_grad = weight_grad(context, out_grad)
    context_grad = linear_back(out_grad, out_block).astype(jnp.bfloat16)
    if keep_mask is not None:
        context_grad = context_grad * keep_mask[:, None, None].astype(jnp.bfloat16)
    probability = jnp.exp(score_block(queries, key_block) - log_total)
    heads_grad = split_heads(context_grad)
    prob_grad = jnp.einsum(
        "pqhe,pkhe->phqk", heads_grad, split_heads(value_block), preferred_element_type=jnp.float32
    )
    value_grad = merge_heads(
        jnp.einsum(
            "phqk,pqhe->pkhe",
            probability.astype(jnp.bfloat16),
            heads_grad,
            preferred_element_type=jnp.float32,
        )
    ).astype(jnp.bfloat16)
    score_grad = (
        probability * (prob_grad - jnp.sum(prob_grad * probability, axis=-1, keepdims=True))
    ).astype(jnp.bfloat16)
    query_grad = (
        merge_heads(
            jnp.einsum(
                "phqk,pkhe->pqhe",
                score_grad,
                split_heads(key_block),
                preferred_element_type=jnp.float32,
            )
        )
        * HEAD ** (-0.5)
    ).astype(jnp.bfloat16)
    key_grad = (
        merge_heads(
            jnp.einsum(
                "phqk,pqhe->pkhe",
                score_grad,
                split_heads(queries),
                preferred_element_type=jnp.float32,
            )
        )
        * HEAD ** (-0.5)
    ).astype(jnp.bfloat16)
    in_weight_grad = jnp.stack(
        [
            weight_grad(query_side, query_grad),
            weight_grad(key_side, key_grad),
            weight_grad(key_side, value_grad),
        ],
        axis=1,
    )
    query_back = linear_back(query_grad, weight_block[:, 0])
    key_back = linear_back(key_grad, weight_block[:, 1]) + linear_back(
        value_grad, weight_block[:, 2]
    )
    return (in_weight_grad, out_weight_grad, query_back, key_back)


def feed_forward(activation, up_block, down_block):
    before = linear(activation, up_block)
    hidden = jax.nn.gelu(before).astype(jnp.bfloat16)
    return (linear(hidden, down_block), (before, hidden))


def feed_back(activation, up_block, down_block, saved, out_grad):
    before, hidden = saved
    down_grad = weight_grad(hidden, out_grad)
    hidden_grad = linear_back(out_grad, down_block)
    gelu_pull = jax.vjp(jax.nn.gelu, before)[1]
    before_grad = gelu_pull(hidden_grad)[0].astype(jnp.bfloat16)
    up_grad = weight_grad(activation, before_grad)
    return (up_grad, down_grad, linear_back(before_grad, up_block))


def per_device(
    text_blocks,
    visual_blocks,
    drop_flags,
    qkv_weight,
    out_weight,
    up_weight,
    down_weight,
    norm_gain,
    norm_shift,
    text_cotangent,
    visual_cotangent,
):
    keep_text = (1 - drop_flags[:, 0]).astype(jnp.float32)
    keep_visual = (1 - drop_flags[:, 1]).astype(jnp.float32)
    text_now = text_blocks.astype(jnp.float32)
    visual_now = visual_blocks.astype(jnp.float32)
    inputs = []
    gathered = []
    saved = []
    for sublayer in range(3):
        inputs.append((text_now, visual_now))
        text_norm = normalize(text_now, norm_gain[2 * sublayer], norm_shift[2 * sublayer]).astype(
            jnp.bfloat16
        )
        visual_norm = normalize(
            visual_now, norm_gain[2 * sublayer + 1], norm_shift[2 * sublayer + 1]
        ).astype(jnp.bfloat16)
        text_rows, visual_rows = (
            lax.all_gather(text_norm, "mp", axis=0, tiled=True),
            lax.all_gather(visual_norm, "mp", axis=0, tiled=True),
        )
        gathered.append((text_rows, visual_rows))
        text_part = None
        visual_part = None
        if sublayer < 2:
            if sublayer == 0:
                text_context, text_saved = attend_context(
                    text_rows, visual_rows, qkv_weight[0], keep_visual
                )
                visual_context, visual_saved = attend_context(
                    visual_rows, text_rows, qkv_weight[1], keep_text
                )
            else:
                text_context, text_saved = attend_context(text_rows, text_rows, qkv_weight[2], None)
                visual_context, visual_saved = attend_context(
                    visual_rows, visual_rows, qkv_weight[3], None
                )
            text_part = linear(text_context, out_weight[2 * sublayer])
            visual_part = linear(visual_context, out_weight[2 * sublayer + 1])
        else:
            text_part, text_saved = feed_forward(text_rows, up_weight[0], down_weight[0])
            visual_part, visual_saved = feed_forward(visual_rows, up_weight[1], down_weight[1])
        text_added, visual_added = (
            lax.psum_scatter(
                text_part.astype(jnp.bfloat16), "mp", scatter_dimension=0, tiled=True
            ).astype(jnp.float32),
            lax.psum_scatter(
                visual_part.astype(jnp.bfloat16), "mp", scatter_dimension=0, tiled=True
            ).astype(jnp.float32),
        )
        saved.append((text_saved, visual_saved))
        text_now = text_now + text_added
        visual_now = visual_now + visual_added
    text_output = text_now.astype(jnp.bfloat16)
    visual_output = visual_now.astype(jnp.bfloat16)
    text_back = text_cotangent.astype(jnp.float32)
    visual_back = visual_cotangent.astype(jnp.float32)
    in_parts = [None, None, None, None]
    out_parts = [None, None, None, None]
    gain_parts = [None, None, None, None, None, None]
    shift_parts = [None, None, None, None, None, None]
    up_grads = None
    down_grads = None
    for sublayer in (2, 1, 0):
        text_branch, visual_branch = (
            lax.all_gather(text_back.astype(jnp.bfloat16), "mp", axis=0, tiled=True),
            lax.all_gather(visual_back.astype(jnp.bfloat16), "mp", axis=0, tiled=True),
        )
        text_rows, visual_rows = gathered[sublayer]
        text_saved, visual_saved = saved[sublayer]
        if sublayer == 2:
            up_text, down_text, text_part = feed_back(
                text_rows, up_weight[0], down_weight[0], text_saved, text_branch
            )
            up_visual, down_visual, visual_part = feed_back(
                visual_rows, up_weight[1], down_weight[1], visual_saved, visual_branch
            )
            up_grads = jnp.stack([up_text, up_visual])
            down_grads = jnp.stack([down_text, down_visual])
        elif sublayer == 1:
            in_parts[2], out_parts[2], query_back, key_back = attend_back(
                text_rows, text_rows, qkv_weight[2], out_weight[2], None, text_saved, text_branch
            )
            text_part = query_back + key_back
            in_parts[3], out_parts[3], query_back, key_back = attend_back(
                visual_rows,
                visual_rows,
                qkv_weight[3],
                out_weight[3],
                None,
                visual_saved,
                visual_branch,
            )
            visual_part = query_back + key_back
        else:
            in_parts[0], out_parts[0], text_query_back, visual_key_back = attend_back(
                text_rows,
                visual_rows,
                qkv_weight[0],
                out_weight[0],
                keep_visual,
                text_saved,
                text_branch,
            )
            in_parts[1], out_parts[1], visual_query_back, text_key_back = attend_back(
                visual_rows,
                text_rows,
                qkv_weight[1],
                out_weight[1],
                keep_text,
                visual_saved,
                visual_branch,
            )
            text_part = text_query_back + text_key_back
            visual_part = visual_query_back + visual_key_back
        text_norm_grad, visual_norm_grad = (
            lax.psum_scatter(
                text_part.astype(jnp.bfloat16), "mp", scatter_dimension=0, tiled=True
            ).astype(jnp.float32),
            lax.psum_scatter(
                visual_part.astype(jnp.bfloat16), "mp", scatter_dimension=0, tiled=True
            ).astype(jnp.float32),
        )
        text_in, visual_in = inputs[sublayer]
        text_pull = jax.vjp(normalize, text_in, norm_gain[2 * sublayer], norm_shift[2 * sublayer])[
            1
        ]
        text_delta, gain_parts[2 * sublayer], shift_parts[2 * sublayer] = text_pull(text_norm_grad)
        visual_pull = jax.vjp(
            normalize, visual_in, norm_gain[2 * sublayer + 1], norm_shift[2 * sublayer + 1]
        )[1]
        visual_delta, gain_parts[2 * sublayer + 1], shift_parts[2 * sublayer + 1] = visual_pull(
            visual_norm_grad
        )
        text_back = text_back + text_delta
        visual_back = visual_back + visual_delta
    gain_grads = jnp.stack(gain_parts)
    shift_grads = jnp.stack(shift_parts)
    gain_grads, shift_grads = (
        lax.psum(gain_grads.astype(jnp.bfloat16), "mp").astype(jnp.float32),
        lax.psum(shift_grads.astype(jnp.bfloat16), "mp").astype(jnp.float32),
    )
    in_grads = jnp.stack(in_parts)
    out_grads = jnp.stack(out_parts)
    in_grads, out_grads, up_grads, down_grads = jax.tree.map(
        lambda grad: lax.psum(grad.astype(jnp.bfloat16), "dp").astype(jnp.float32),
        (in_grads, out_grads, up_grads, down_grads),
    )
    gain_grads, shift_grads = lax.psum((gain_grads, shift_grads), "dp")
    return (
        text_output,
        visual_output,
        text_back.astype(jnp.bfloat16),
        visual_back.astype(jnp.bfloat16),
        in_grads,
        out_grads,
        up_grads,
        down_grads,
        gain_grads,
        shift_grads,
    )


def solution(mesh):
    placed = (
        P(("dp", "mp"), None, None),
        P(("dp", "mp"), None, None),
        P("dp", None),
        P(None, None, None, "mp"),
        P(None, "mp", None),
        P(None, None, "mp"),
        P(None, "mp", None),
        P(),
        P(),
        P(("dp", "mp"), None, None),
        P(("dp", "mp"), None, None),
    )
    return jax.shard_map(
        per_device,
        mesh=mesh,
        in_specs=placed,
        out_specs=(
            P(("dp", "mp"), None, None),
            P(("dp", "mp"), None, None),
            P(("dp", "mp"), None, None),
            P(("dp", "mp"), None, None),
            P(None, None, None, "mp"),
            P(None, "mp", None),
            P(None, None, "mp"),
            P(None, "mp", None),
            P(),
            P(),
        ),
        check_vma=False,
    )
```

```python
import jax
import jax.numpy as jnp
from jax import lax
from jax.experimental import pallas as pl
from jax.experimental.pallas import tpu as pltpu
from jax.sharding import PartitionSpec as P

HEAD = 64
EPSILON = 1e-05
CHUNKS = 2
NEG = -1e30
GELU_A = 0.7978845608028654
GELU_B = 0.044715
F32 = jnp.float32
BF16 = jnp.bfloat16


def dot_nn(a, b):
    return lax.dot_general(a, b, (((1,), (0,)), ((), ())), preferred_element_type=F32)


def dot_nt(a, b):
    return lax.dot_general(a, b, (((1,), (1,)), ((), ())), preferred_element_type=F32)


def dot_tn(a, b):
    return lax.dot_general(a, b, (((0,), (0,)), ((), ())), preferred_element_type=F32)


def head_masks(width, scale):
    lane = lax.broadcasted_iota(jnp.int32, (1, width), 1)
    return [
        jnp.where(lane // HEAD == head, scale, 0.0).astype(BF16) for head in range(width // HEAD)
    ]


def page_bias(rows, row_len, cols, col_len):
    row = lax.broadcasted_iota(jnp.int32, (rows, cols), 0) >= row_len
    col = lax.broadcasted_iota(jnp.int32, (rows, cols), 1) >= col_len
    return jnp.where(row == col, 0.0, NEG).astype(F32)


def softmax(scores):
    top = jnp.max(scores, axis=-1, keepdims=True)
    weight = jnp.exp(scores - top)
    return weight * (1.0 / jnp.sum(weight, axis=-1, keepdims=True))


def spans(tlen, vlen, pages):
    out = []
    for pair in range(pages // 2):
        text = (2 * tlen * pair, 2 * tlen, tlen)
        visual = (tlen * pages + 2 * vlen * pair, 2 * vlen, vlen)
        out.append((text, visual))
    return out


def attend_kernel(cross, tlen, vlen, pages, *refs):
    if cross:
        n_ref, w_ref, wo_ref, keep_ref, part_ref, saved_ref = refs
    else:
        n_ref, w_ref, wo_ref, part_ref, saved_ref = refs
    width = wo_ref.shape[1]
    trows = tlen * pages
    rows = trows + vlen * pages
    sides = (slice(0, trows), slice(trows, rows))
    for stream, side in enumerate(sides):
        block = n_ref[0, side, :]
        for kind in range(3):
            saved_ref[0, kind, side, :] = dot_nn(block, w_ref[stream, kind]).astype(BF16)
    scaled = head_masks(width, HEAD**-0.5)
    plain = head_masks(width, 1.0)
    for text, visual in spans(tlen, vlen, pages):
        for query, own, other in ((text, text, visual), (visual, visual, text)):
            key = other if cross else own
            bias = page_bias(query[1], query[2], key[1], key[2])
            qs = slice(query[0], query[0] + query[1])
            ks = slice(key[0], key[0] + key[1])
            q = saved_ref[0, 0, qs, :]
            k = saved_ref[0, 1, ks, :]
            v = saved_ref[0, 2, ks, :]
            context = None
            for head in range(width // HEAD):
                probs = softmax(dot_nt(q * scaled[head], k) + bias).astype(BF16)
                term = dot_nn(probs, v * plain[head])
                context = term if context is None else context + term
            if cross:
                context = context * keep_ref[0, qs, :]
            saved_ref[0, 3, qs, :] = context.astype(BF16)
    for stream, side in enumerate(sides):
        part_ref[0, side, :] = dot_nn(saved_ref[0, 3, side, :], wo_ref[stream]).astype(BF16)


def attend_back_kernel(cross, tlen, vlen, pages, *refs):
    if cross:
        n_ref, gy_ref, saved_ref, w_ref, wo_ref, keep_ref, part_ref, grad_ref, gc, d, acc = refs
    else:
        n_ref, gy_ref, saved_ref, w_ref, wo_ref, part_ref, grad_ref, gc, d, acc = refs
    step = pl.program_id(0)
    width = wo_ref.shape[1]
    trows = tlen * pages
    rows = trows + vlen * pages
    sides = (slice(0, trows), slice(trows, rows))

    @pl.when(step == 0)
    def _():
        acc[...] = jnp.zeros_like(acc)

    for stream, side in enumerate(sides):
        gy = gy_ref[0, side, :]
        grad = dot_nt(gy, wo_ref[stream]).astype(BF16)
        if cross:
            grad = grad * keep_ref[0, side, :].astype(BF16)
        gc[side, :] = grad
        at = (6 + stream) * width
        acc[at : at + width, :] += dot_tn(saved_ref[0, 3, side, :], gy)
    scaled = head_masks(width, HEAD**-0.5)
    plain = head_masks(width, 1.0)
    for text, visual in spans(tlen, vlen, pages):
        for query, own, other in ((text, text, visual), (visual, visual, text)):
            key = other if cross else own
            bias = page_bias(query[1], query[2], key[1], key[2])
            qs = slice(query[0], query[0] + query[1])
            ks = slice(key[0], key[0] + key[1])
            q = saved_ref[0, 0, qs, :]
            k = saved_ref[0, 1, ks, :]
            v = saved_ref[0, 2, ks, :]
            g = gc[qs, :]
            dq = dk = dv = 0.0
            for head in range(width // HEAD):
                q_head = q * scaled[head]
                g_head = g * plain[head]
                p = softmax(dot_nt(q_head, k) + bias)
                gp = dot_nt(g_head, v)
                gs = (p * (gp - jnp.sum(gp * p, axis=-1, keepdims=True))).astype(BF16)
                dv += dot_tn(p.astype(BF16), g_head)
                dq += dot_nn(gs, k * scaled[head])
                dk += dot_tn(gs, q_head)
            d[0, qs, :] = dq.astype(BF16)
            d[1, ks, :] = dk.astype(BF16)
            d[2, ks, :] = dv.astype(BF16)
    for stream, side in enumerate(sides):
        block = n_ref[0, side, :]
        part = None
        for kind in range(3):
            grad = d[kind, side, :]
            term = dot_nt(grad, w_ref[stream, kind])
            part = term if part is None else part + term
            at = (3 * stream + kind) * width
            acc[at : at + width, :] += dot_tn(grad, block)
        part_ref[0, side, :] = part.astype(BF16)

    @pl.when(step == pl.num_programs(0) - 1)
    def _():
        grad_ref[...] = acc[...].astype(BF16)


def feed_kernel(trows, *refs):
    n_ref, gy_ref, up_ref, down_ref, out_ref, part_ref, grad_ref, acc = refs
    step = pl.program_id(0)
    rows = n_ref.shape[1]
    depth = up_ref.shape[1]
    hid = up_ref.shape[2]

    @pl.when(step == 0)
    def _():
        acc[...] = jnp.zeros_like(acc)

    for stream, side in enumerate((slice(0, trows), slice(trows, rows))):
        block = n_ref[0, side, :]
        gy = gy_ref[0, side, :]
        pre = dot_nn(block, up_ref[stream])
        square = pre * pre
        bent = jnp.tanh(GELU_A * (pre + GELU_B * (square * pre)))
        half = 0.5 * (1.0 + bent)
        hidden = (pre * half).astype(BF16)
        slope = half + 0.5 * pre * (1.0 - bent * bent) * (GELU_A * (1.0 + 3.0 * GELU_B * square))
        out_ref[0, side, :] = dot_nn(hidden, down_ref[stream]).astype(BF16)
        g_pre = (dot_nt(gy, down_ref[stream]) * slope).astype(BF16)
        part_ref[0, side, :] = dot_nt(g_pre, up_ref[stream]).astype(BF16)
        at = stream * depth
        acc[at : at + depth, :] += dot_tn(block, g_pre)
        at = 2 * depth + stream * hid
        acc[at : at + hid, :] += dot_tn(hidden, gy)

    @pl.when(step == pl.num_programs(0) - 1)
    def _():
        grad_ref[...] = acc[...].astype(BF16)


def per_block(shape):
    return pl.BlockSpec((1,) + shape[1:], lambda i: (i,) + (0,) * (len(shape) - 1))


def whole(shape):
    return pl.BlockSpec(shape, lambda i: (0,) * len(shape))


def cost(flops, arrays):
    size = sum(a.size * a.dtype.itemsize for a in arrays)
    return pl.CostEstimate(flops=int(flops), bytes_accessed=int(size), transcendentals=0)


def attend(rows_all, weights, out_weights, keep, tlen, vlen, pages):
    blocks, rows, depth = rows_all.shape
    width = out_weights.shape[1]
    args = [rows_all, weights, out_weights]
    specs = [per_block(rows_all.shape), whole(weights.shape), whole(out_weights.shape)]
    if keep is not None:
        args.append(keep)
        specs.append(per_block(keep.shape))
    outs = (
        jax.ShapeDtypeStruct((blocks, rows, depth), BF16),
        jax.ShapeDtypeStruct((blocks, 4, rows, width), BF16),
    )

    def body(*refs):
        attend_kernel(keep is not None, tlen, vlen, pages, *refs)

    return pl.pallas_call(
        body,
        grid=(blocks,),
        in_specs=specs,
        out_specs=tuple(per_block(o.shape) for o in outs),
        out_shape=outs,
        cost_estimate=cost(2 * blocks * rows * (4 * depth * width + 1536 * width), args + list(outs)),
        name="attend_cross" if keep is not None else "attend_self",
    )(*args)


def attend_back(rows_all, grad_all, saved, weights, out_weights, keep, tlen, vlen, pages):
    blocks, rows, depth = rows_all.shape
    width = out_weights.shape[1]
    args = [rows_all, grad_all, saved, weights, out_weights]
    specs = [per_block(a.shape) for a in args[:3]] + [whole(a.shape) for a in args[3:]]
    if keep is not None:
        args.append(keep)
        specs.append(per_block(keep.shape))
    outs = (
        jax.ShapeDtypeStruct((blocks, rows, depth), BF16),
        jax.ShapeDtypeStruct((8 * width, depth), BF16),
    )

    def body(*refs):
        attend_back_kernel(keep is not None, tlen, vlen, pages, *refs)

    return pl.pallas_call(
        body,
        grid=(blocks,),
        in_specs=specs,
        out_specs=(per_block(outs[0].shape), whole(outs[1].shape)),
        out_shape=outs,
        scratch_shapes=[
            pltpu.VMEM((rows, width), BF16),
            pltpu.VMEM((3, rows, width), BF16),
            pltpu.VMEM((8 * width, depth), F32),
        ],
        cost_estimate=cost(2 * blocks * rows * (8 * depth * width + 4096 * width), args + list(outs)),
        name="attend_cross_back" if keep is not None else "attend_self_back",
    )(*args)


def feed(rows_all, grad_all, up, down, trows):
    blocks, rows, depth = rows_all.shape
    hid = up.shape[2]
    args = [rows_all, grad_all, up, down]
    outs = (
        jax.ShapeDtypeStruct((blocks, rows, depth), BF16),
        jax.ShapeDtypeStruct((blocks, rows, depth), BF16),
        jax.ShapeDtypeStruct((2 * depth + 2 * hid, depth), BF16),
    )

    def body(*refs):
        feed_kernel(trows, *refs)

    return pl.pallas_call(
        body,
        grid=(blocks,),
        in_specs=[per_block(a.shape) for a in args[:2]] + [whole(a.shape) for a in args[2:]],
        out_specs=(per_block(outs[0].shape), per_block(outs[1].shape), whole(outs[2].shape)),
        out_shape=outs,
        scratch_shapes=[pltpu.VMEM((2 * depth + 2 * hid, depth), F32)],
        cost_estimate=cost(2 * blocks * rows * 6 * depth * hid, args + list(outs)),
        name="feed_both",
    )(*args)


def swap(values, axis, bit, size):
    return lax.ppermute(values, axis, [(i, i ^ bit) for i in range(size)])


def gather_rows(values):
    pair = jnp.stack([values, swap(values, "mp", 2, 4)])
    return jnp.concatenate([pair, swap(pair, "mp", 1, 4)])


def scatter_rows(parts):
    pair = parts[:2].astype(F32) + swap(parts[2:], "mp", 1, 4).astype(F32)
    return pair[0] + swap(pair[1].astype(BF16), "mp", 2, 4).astype(F32)


def moments(values):
    center = values - jnp.mean(values, axis=-1, keepdims=True)
    spread = jnp.mean(center * center, axis=-1, keepdims=True)
    inverse = lax.rsqrt(spread + EPSILON)
    return center * inverse, inverse


def normalize(values, gain, shift):
    return (moments(values)[0] * gain + shift).astype(BF16)


def normalize_back(values, gain, grad):
    scaled, inverse = moments(values)
    inner = grad * gain
    delta = inverse * (
        inner
        - jnp.mean(inner, axis=-1, keepdims=True)
        - scaled * jnp.mean(inner * scaled, axis=-1, keepdims=True)
    )
    return delta, grad * scaled


def reduce_grads(grads, count):
    total = lax.psum(grads, "dp")
    return total.astype(F32)


def per_device(count, *arrays):
    (
        text_blocks,
        visual_blocks,
        drop_flags,
        qkv_weight,
        out_weight,
        up_weight,
        down_weight,
        norm_gain,
        norm_shift,
        text_cotangent,
        visual_cotangent,
    ) = arrays
    local, tlen, depth = text_blocks.shape
    vlen = visual_blocks.shape[1]
    width = out_weight.shape[1]
    pages = local // CHUNKS
    trows, vrows = pages * tlen, pages * vlen
    rows = trows + vrows

    def join(text, visual):
        text = text.reshape(CHUNKS, trows, depth)
        visual = visual.reshape(CHUNKS, vrows, depth)
        return [jnp.concatenate([text[c], visual[c]]) for c in range(CHUNKS)]

    def part(values):
        text = jnp.stack([v[:trows] for v in values]).reshape(local, tlen, depth)
        visual = jnp.stack([v[trows:] for v in values]).reshape(local, vlen, depth)
        return text.astype(BF16), visual.astype(BF16)

    def row_wise(pairs):
        is_text = lax.broadcasted_iota(jnp.int32, (rows, 1), 0) < trows
        return jnp.where(is_text, pairs[0], pairs[1])

    me = lax.axis_index("mp")
    order = me ^ jnp.array([0, 2, 1, 3], jnp.int32)
    keep = (1 - drop_flags).astype(F32).reshape(4, CHUNKS, pages, 2)[order]
    keep_rows = []
    for c in range(CHUNKS):
        text = jnp.repeat(keep[:, c, :, 1], tlen, axis=1)
        visual = jnp.repeat(keep[:, c, :, 0], vlen, axis=1)
        keep_rows.append(jnp.concatenate([text, visual], axis=1)[:, :, None])

    kinds = jnp.transpose(qkv_weight, (0, 2, 1, 3))
    cross_weights = jnp.stack(
        [
            jnp.stack([kinds[0, 0], kinds[1, 1], kinds[1, 2]]),
            jnp.stack([kinds[1, 0], kinds[0, 1], kinds[0, 2]]),
        ]
    )
    self_weights = kinds[2:]
    weights = (cross_weights, self_weights)
    outs = (out_weight[:2], out_weight[2:])
    gains = [row_wise((norm_gain[2 * s], norm_gain[2 * s + 1])) for s in range(3)]
    shifts = [row_wise((norm_shift[2 * s], norm_shift[2 * s + 1])) for s in range(3)]

    now = [v.astype(F32) for v in join(text_blocks, visual_blocks)]
    cotangents = join(text_cotangent, visual_cotangent)
    inputs = [list(now), None, None]
    gathered = [[None] * CHUNKS for _ in range(3)]
    saved = [[None] * CHUNKS for _ in range(2)]
    for s in range(2):
        for c in range(CHUNKS):
            gathered[s][c] = gather_rows(normalize(now[c], gains[s], shifts[s]))
            parts, saved[s][c] = attend(
                gathered[s][c],
                weights[s],
                outs[s],
                keep_rows[c] if s == 0 else None,
                tlen,
                vlen,
                pages,
            )
            now[c] = now[c] + scatter_rows(parts)
        inputs[s + 1] = list(now)
    grads_now = [v.astype(F32) for v in cotangents]
    totals = [None] * 3
    scale_sums = [None] * 3
    shift_sums = [None] * 3

    def back(s, c, parts):
        grad = scatter_rows(parts)
        delta, product = normalize_back(inputs[s][c], gains[s], grad)
        grads_now[c] = grads_now[c] + delta
        sums = [jnp.sum(v, axis=0) for v in (product[:trows], product[trows:])]
        shifts = [jnp.sum(v, axis=0) for v in (grad[:trows], grad[trows:])]
        sums, shifts = jnp.stack(sums), jnp.stack(shifts)
        scale_sums[s] = sums if scale_sums[s] is None else scale_sums[s] + sums
        shift_sums[s] = shifts if shift_sums[s] is None else shift_sums[s] + shifts

    partial = []
    for c in range(CHUNKS):
        cot = gather_rows(cotangents[c])
        rows_all = gather_rows(normalize(now[c], gains[2], shifts[2]))
        out, parts, grads = feed(rows_all, cot, up_weight, down_weight, trows)
        partial.append(grads.astype(F32))
        back(2, c, parts)
        now[c] = now[c] + scatter_rows(out)
    totals[2] = reduce_grads(sum(partial).astype(BF16), count)
    for s in (1, 0):
        partial = []
        for c in range(CHUNKS):
            grad_all = gather_rows(grads_now[c].astype(BF16))
            parts, grads = attend_back(
                gathered[s][c],
                grad_all,
                saved[s][c],
                weights[s],
                outs[s],
                keep_rows[c] if s == 0 else None,
                tlen,
                vlen,
                pages,
            )
            partial.append(grads.astype(F32))
            back(s, c, parts)
        totals[s] = reduce_grads(sum(partial).astype(BF16), count)

    small = jnp.concatenate(scale_sums + shift_sums)
    for bit in (1, 2):
        small = small + swap(small, "mp", bit, 4)
    bit = 1
    while bit < count:
        small = small + swap(small, "dp", bit, count)
        bit *= 2

    text_output, visual_output = part(now)
    text_gradient, visual_gradient = part(grads_now)
    in_parts = [t[: 6 * width].reshape(2, 3, width, depth) for t in totals[:2]]
    cross = in_parts[0]
    cross = jnp.stack(
        [
            jnp.stack([cross[0, 0], cross[1, 1], cross[1, 2]]),
            jnp.stack([cross[1, 0], cross[0, 1], cross[0, 2]]),
        ]
    )
    in_grads = jnp.transpose(jnp.concatenate([cross, in_parts[1]]), (0, 3, 1, 2))
    out_grads = jnp.concatenate([t[6 * width :].reshape(2, width, depth) for t in totals[:2]])
    hid = up_weight.shape[2]
    up_grads = totals[2][: 2 * depth].reshape(2, depth, hid)
    down_grads = totals[2][2 * depth :].reshape(2, hid, depth)
    return (
        text_output,
        visual_output,
        text_gradient,
        visual_gradient,
        in_grads,
        out_grads,
        up_grads,
        down_grads,
        small[:6],
        small[6:],
    )


def solution(mesh):
    placed = (
        P(("dp", "mp"), None, None),
        P(("dp", "mp"), None, None),
        P("dp", None),
        P(None, None, None, "mp"),
        P(None, "mp", None),
        P(None, None, "mp"),
        P(None, "mp", None),
        P(),
        P(),
        P(("dp", "mp"), None, None),
        P(("dp", "mp"), None, None),
    )
    count = mesh.shape["dp"]

    def device(*arrays):
        return per_device(count, *arrays)

    return jax.shard_map(
        device,
        mesh=mesh,
        in_specs=placed,
        out_specs=(
            P(("dp", "mp"), None, None),
            P(("dp", "mp"), None, None),
            P(("dp", "mp"), None, None),
            P(("dp", "mp"), None, None),
            P(None, None, None, "mp"),
            P(None, "mp", None),
            P(None, None, "mp"),
            P(None, "mp", None),
            P(),
            P(),
        ),
        check_vma=False,
    )
```

```python
import jax
import jax.numpy as jnp
from jax import lax
from jax.experimental import pallas as pl
from jax.experimental.pallas import tpu as pltpu
from jax.sharding import PartitionSpec as P

HEAD = 64
EPSILON = 1e-05
CHUNKS = 2
NEG = -1e30
GELU_A = 0.7978845608028654
GELU_B = 0.044715
F32 = jnp.float32
BF16 = jnp.bfloat16


def dot_nn(a, b):
    return lax.dot_general(a, b, (((1,), (0,)), ((), ())), preferred_element_type=F32)


def dot_nt(a, b):
    return lax.dot_general(a, b, (((1,), (1,)), ((), ())), preferred_element_type=F32)


def dot_tn(a, b):
    return lax.dot_general(a, b, (((0,), (0,)), ((), ())), preferred_element_type=F32)


def head_masks(width, scale):
    lane = lax.broadcasted_iota(jnp.int32, (1, width), 1)
    return [
        jnp.where(lane // HEAD == head, scale, 0.0).astype(BF16) for head in range(width // HEAD)
    ]


def page_bias(rows, row_len, cols, col_len):
    row = lax.broadcasted_iota(jnp.int32, (rows, cols), 0) >= row_len
    col = lax.broadcasted_iota(jnp.int32, (rows, cols), 1) >= col_len
    return jnp.where(row == col, 0.0, NEG).astype(F32)


def softmax(scores):
    top = jnp.max(scores, axis=-1, keepdims=True)
    weight = jnp.exp(scores - top)
    return weight * (1.0 / jnp.sum(weight, axis=-1, keepdims=True))


def spans(tlen, vlen, pages):
    out = []
    for pair in range(pages // 2):
        text = (2 * tlen * pair, 2 * tlen, tlen)
        visual = (tlen * pages + 2 * vlen * pair, 2 * vlen, vlen)
        out.append((text, visual))
    return out


def pick(step, refs, block):
    for at, ref in enumerate(refs):

        @pl.when(step == at)
        def _():
            block[...] = ref[...]


def place(step, refs, block):
    for at, ref in enumerate(refs):

        @pl.when(step == at)
        def _():
            ref[...] = block[...]


def attend_kernel(cross, tlen, vlen, pages, *refs):
    n_refs, refs = refs[:4], refs[4:]
    if cross:
        w_ref, wo_ref, keep_ref, *part_refs, saved_ref, n, part = refs
    else:
        w_ref, wo_ref, *part_refs, saved_ref, n, part = refs
    step = pl.program_id(0)
    pick(step, n_refs, n)
    width = wo_ref.shape[1]
    trows = tlen * pages
    rows = trows + vlen * pages
    sides = (slice(0, trows), slice(trows, rows))
    for stream, side in enumerate(sides):
        block = n[side, :]
        for kind in range(3):
            saved_ref[0, kind, side, :] = dot_nn(block, w_ref[stream, kind]).astype(BF16)
    scaled = head_masks(width, HEAD**-0.5)
    plain = head_masks(width, 1.0)
    for text, visual in spans(tlen, vlen, pages):
        for query, own, other in ((text, text, visual), (visual, visual, text)):
            key = other if cross else own
            bias = page_bias(query[1], query[2], key[1], key[2])
            qs = slice(query[0], query[0] + query[1])
            ks = slice(key[0], key[0] + key[1])
            q = saved_ref[0, 0, qs, :]
            k = saved_ref[0, 1, ks, :]
            v = saved_ref[0, 2, ks, :]
            context = None
            for head in range(width // HEAD):
                probs = softmax(dot_nt(q * scaled[head], k) + bias).astype(BF16)
                term = dot_nn(probs, v * plain[head])
                context = term if context is None else context + term
            if cross:
                context = context * keep_ref[0, qs, :]
            saved_ref[0, 3, qs, :] = context.astype(BF16)
    for stream, side in enumerate(sides):
        part[side, :] = dot_nn(saved_ref[0, 3, side, :], wo_ref[stream]).astype(BF16)
    place(step, part_refs, part)


def attend_back_kernel(cross, tlen, vlen, pages, *refs):
    n_refs, gy_refs, refs = refs[:4], refs[4:8], refs[8:]
    if cross:
        saved_ref, w_ref, wo_ref, keep_ref, *part_refs, grad_ref, n, gy_all, gc, d, acc = refs
    else:
        saved_ref, w_ref, wo_ref, *part_refs, grad_ref, n, gy_all, gc, d, acc = refs
    step = pl.program_id(0)
    pick(step, n_refs, n)
    pick(step, gy_refs, gy_all)
    width = wo_ref.shape[1]
    trows = tlen * pages
    rows = trows + vlen * pages
    sides = (slice(0, trows), slice(trows, rows))

    @pl.when(step == 0)
    def _():
        acc[...] = jnp.zeros_like(acc)

    for stream, side in enumerate(sides):
        gy = gy_all[side, :]
        grad = dot_nt(gy, wo_ref[stream]).astype(BF16)
        if cross:
            grad = grad * keep_ref[0, side, :].astype(BF16)
        gc[side, :] = grad
        at = (6 + stream) * width
        acc[at : at + width, :] += dot_tn(saved_ref[0, 3, side, :], gy)
    scaled = head_masks(width, HEAD**-0.5)
    plain = head_masks(width, 1.0)
    for text, visual in spans(tlen, vlen, pages):
        for query, own, other in ((text, text, visual), (visual, visual, text)):
            key = other if cross else own
            bias = page_bias(query[1], query[2], key[1], key[2])
            qs = slice(query[0], query[0] + query[1])
            ks = slice(key[0], key[0] + key[1])
            q = saved_ref[0, 0, qs, :]
            k = saved_ref[0, 1, ks, :]
            v = saved_ref[0, 2, ks, :]
            g = gc[qs, :]
            dq = dk = dv = 0.0
            for head in range(width // HEAD):
                q_head = q * scaled[head]
                g_head = g * plain[head]
                p = softmax(dot_nt(q_head, k) + bias)
                gp = dot_nt(g_head, v)
                gs = (p * (gp - jnp.sum(gp * p, axis=-1, keepdims=True))).astype(BF16)
                dv += dot_tn(p.astype(BF16), g_head)
                dq += dot_nn(gs, k * scaled[head])
                dk += dot_tn(gs, q_head)
            d[0, qs, :] = dq.astype(BF16)
            d[1, ks, :] = dk.astype(BF16)
            d[2, ks, :] = dv.astype(BF16)
    for stream, side in enumerate(sides):
        block = n[side, :]
        part = None
        for kind in range(3):
            grad = d[kind, side, :]
            term = dot_nt(grad, w_ref[stream, kind])
            part = term if part is None else part + term
            at = (3 * stream + kind) * width
            acc[at : at + width, :] += dot_tn(grad, block)
        gy_all[side, :] = part.astype(BF16)
    place(step, part_refs, gy_all)

    @pl.when(step == pl.num_programs(0) - 1)
    def _():
        grad_ref[...] = acc[...].astype(BF16)


def feed_kernel(trows, *refs):
    n_refs, gy_refs, refs = refs[:4], refs[4:8], refs[8:]
    up_ref, down_ref, refs = refs[0], refs[1], refs[2:]
    out_refs, part_refs, refs = refs[:4], refs[4:8], refs[8:]
    grad_ref, n, gy_all, out, part, acc = refs
    step = pl.program_id(0)
    pick(step, n_refs, n)
    pick(step, gy_refs, gy_all)
    rows = n.shape[0]
    depth = up_ref.shape[1]
    hid = up_ref.shape[2]

    @pl.when(step == 0)
    def _():
        acc[...] = jnp.zeros_like(acc)

    for stream, side in enumerate((slice(0, trows), slice(trows, rows))):
        block = n[side, :]
        gy = gy_all[side, :]
        pre = dot_nn(block, up_ref[stream])
        square = pre * pre
        bent = jnp.tanh(GELU_A * (pre + GELU_B * (square * pre)))
        half = 0.5 * (1.0 + bent)
        hidden = (pre * half).astype(BF16)
        slope = half + 0.5 * pre * (1.0 - bent * bent) * (GELU_A * (1.0 + 3.0 * GELU_B * square))
        out[side, :] = dot_nn(hidden, down_ref[stream]).astype(BF16)
        g_pre = (dot_nt(gy, down_ref[stream]) * slope).astype(BF16)
        part[side, :] = dot_nt(g_pre, up_ref[stream]).astype(BF16)
        at = stream * depth
        acc[at : at + depth, :] += dot_tn(block, g_pre)
        at = 2 * depth + stream * hid
        acc[at : at + hid, :] += dot_tn(hidden, gy)
    place(step, out_refs, out)
    place(step, part_refs, part)

    @pl.when(step == pl.num_programs(0) - 1)
    def _():
        grad_ref[...] = acc[...].astype(BF16)


def per_block(shape):
    return pl.BlockSpec((1,) + shape[1:], lambda i: (i,) + (0,) * (len(shape) - 1))


def whole(shape):
    return pl.BlockSpec(shape, lambda i: (0,) * len(shape))


def cost(flops, arrays):
    size = sum(a.size * a.dtype.itemsize for a in arrays)
    return pl.CostEstimate(flops=int(flops), bytes_accessed=int(size), transcendentals=0)


def attend(blocks, weights, out_weights, keep, tlen, vlen, pages):
    rows, depth = blocks[0].shape
    width = out_weights.shape[1]
    args = [*blocks, weights, out_weights]
    specs = [whole(a.shape) for a in args]
    if keep is not None:
        args.append(keep)
        specs.append(per_block(keep.shape))
    outs = [jax.ShapeDtypeStruct((rows, depth), BF16)] * 4
    outs.append(jax.ShapeDtypeStruct((4, 4, rows, width), BF16))

    def body(*refs):
        attend_kernel(keep is not None, tlen, vlen, pages, *refs)

    *parts, saved = pl.pallas_call(
        body,
        grid=(4,),
        in_specs=specs,
        out_specs=[whole(o.shape) for o in outs[:4]] + [per_block(outs[4].shape)],
        out_shape=outs,
        scratch_shapes=[pltpu.VMEM((rows, depth), BF16)] * 2,
        cost_estimate=cost(8 * rows * (4 * depth * width + 1536 * width), args + outs),
        name="attend_cross" if keep is not None else "attend_self",
    )(*args)
    return parts, saved


def attend_back(blocks, grad_blocks, saved, weights, out_weights, keep, tlen, vlen, pages):
    rows, depth = blocks[0].shape
    width = out_weights.shape[1]
    args = [*blocks, *grad_blocks, saved, weights, out_weights]
    specs = [whole(a.shape) for a in args]
    specs[8] = per_block(saved.shape)
    if keep is not None:
        args.append(keep)
        specs.append(per_block(keep.shape))
    outs = [jax.ShapeDtypeStruct((rows, depth), BF16)] * 4
    outs.append(jax.ShapeDtypeStruct((8 * width, depth), BF16))

    def body(*refs):
        attend_back_kernel(keep is not None, tlen, vlen, pages, *refs)

    *parts, grads = pl.pallas_call(
        body,
        grid=(4,),
        in_specs=specs,
        out_specs=[whole(o.shape) for o in outs],
        out_shape=outs,
        scratch_shapes=[
            pltpu.VMEM((rows, depth), BF16),
            pltpu.VMEM((rows, depth), BF16),
            pltpu.VMEM((rows, width), BF16),
            pltpu.VMEM((3, rows, width), BF16),
            pltpu.VMEM((8 * width, depth), F32),
        ],
        cost_estimate=cost(8 * rows * (8 * depth * width + 4096 * width), args + outs),
        name="attend_cross_back" if keep is not None else "attend_self_back",
    )(*args)
    return parts, grads


def feed(blocks, grad_blocks, up, down, trows):
    rows, depth = blocks[0].shape
    hid = up.shape[2]
    args = [*blocks, *grad_blocks, up, down]
    outs = [jax.ShapeDtypeStruct((rows, depth), BF16)] * 8
    outs.append(jax.ShapeDtypeStruct((2 * depth + 2 * hid, depth), BF16))

    def body(*refs):
        feed_kernel(trows, *refs)

    results = pl.pallas_call(
        body,
        grid=(4,),
        in_specs=[whole(a.shape) for a in args],
        out_specs=[whole(o.shape) for o in outs],
        out_shape=outs,
        scratch_shapes=[pltpu.VMEM((rows, depth), BF16)] * 4
        + [pltpu.VMEM((2 * depth + 2 * hid, depth), F32)],
        cost_estimate=cost(8 * rows * 6 * depth * hid, args + outs),
        name="feed_both",
    )(*args)
    return results[:4], results[4:8], results[8]


def swap(values, axis, bit, size):
    return lax.ppermute(values, axis, [(i, i ^ bit) for i in range(size)])


def after(values, *earlier):
    earlier = [e for e in earlier if e is not None]
    if not earlier:
        return values
    return lax.optimization_barrier((values, earlier))[0]


def gather_start(values):
    return values, swap(values, "mp", 2, 4), swap(values, "mp", 1, 4)


def gather_end(started, *earlier):
    values, far, near = started
    far = after(far, *earlier)
    return [values, far, near, swap(far, "mp", 1, 4)]


def scatter_start(parts):
    own, far, near, both = parts
    send = (far.astype(F32) + swap(both, "mp", 1, 4).astype(F32)).astype(BF16)
    return own, swap(near, "mp", 1, 4), swap(send, "mp", 2, 4), send


def scatter_end(started, *earlier):
    own, near, far, _ = started
    far = after(far, *earlier)
    return own.astype(F32) + near.astype(F32) + far.astype(F32)


def moments(values):
    center = values - jnp.mean(values, axis=-1, keepdims=True)
    spread = jnp.mean(center * center, axis=-1, keepdims=True)
    inverse = lax.rsqrt(spread + EPSILON)
    return center * inverse, inverse


def normalize(values, gain, shift):
    return (moments(values)[0] * gain + shift).astype(BF16)


def normalize_back(values, gain, grad):
    scaled, inverse = moments(values)
    inner = grad * gain
    delta = inverse * (
        inner
        - jnp.mean(inner, axis=-1, keepdims=True)
        - scaled * jnp.mean(inner * scaled, axis=-1, keepdims=True)
    )
    return delta, grad * scaled


class Ring:
    def __init__(self, grads, count):
        self.shape, self.count = grads.shape, count
        self.mine = lax.psum_scatter(grads, "dp", scatter_dimension=0, tiled=True)
        self.right = self.left = self.mine
        self.hops = 0
        self.pieces = [(self.mine, 0)]
        self.order = list(range(0, count, 2)) + list(range(count - 1, 0, -2))

    def hop(self):
        order, count = self.order, self.count
        if self.hops >= count // 2:
            return
        self.hops += 1
        onward = [(order[k], order[(k + 1) % count]) for k in range(count)]
        self.right = lax.ppermute(self.right, "dp", onward)
        self.pieces.append((self.right, count - self.hops))
        if self.hops < count - count // 2:
            self.left = lax.ppermute(self.left, "dp", [(b, a) for a, b in onward])
            self.pieces.append((self.left, self.hops))

    def state(self):
        return (self.right, self.left)

    def total(self):
        while self.hops < self.count // 2:
            self.hop()
        at = lax.axis_index("dp")
        position = jnp.array([self.order.index(i) for i in range(self.count)], jnp.int32)[at]
        device_at = jnp.array(self.order, jnp.int32)
        total = jnp.zeros(self.shape, F32)
        length = self.mine.shape[0]
        for piece, offset in self.pieces:
            row = device_at[(position + offset) % self.count] * length
            total = lax.dynamic_update_slice(total, piece.astype(F32), (row, 0))
        return total


def per_device(count, *arrays):
    (
        text_blocks,
        visual_blocks,
        drop_flags,
        qkv_weight,
        out_weight,
        up_weight,
        down_weight,
        norm_gain,
        norm_shift,
        text_cotangent,
        visual_cotangent,
    ) = arrays
    local, tlen, depth = text_blocks.shape
    vlen = visual_blocks.shape[1]
    width = out_weight.shape[1]
    pages = local // CHUNKS
    trows, vrows = pages * tlen, pages * vlen
    rows = trows + vrows

    def join(text, visual):
        text = text.reshape(CHUNKS, trows, depth)
        visual = visual.reshape(CHUNKS, vrows, depth)
        return [jnp.concatenate([text[c], visual[c]]) for c in range(CHUNKS)]

    def part(values):
        text = jnp.stack([v[:trows] for v in values]).reshape(local, tlen, depth)
        visual = jnp.stack([v[trows:] for v in values]).reshape(local, vlen, depth)
        return text.astype(BF16), visual.astype(BF16)

    def row_wise(pairs):
        is_text = lax.broadcasted_iota(jnp.int32, (rows, 1), 0) < trows
        return jnp.where(is_text, pairs[0], pairs[1])

    me = lax.axis_index("mp")
    order = me ^ jnp.array([0, 2, 1, 3], jnp.int32)
    keep = (1 - drop_flags).astype(F32).reshape(4, CHUNKS, pages, 2)[order]
    keep_rows = []
    for c in range(CHUNKS):
        text = jnp.repeat(keep[:, c, :, 1], tlen, axis=1)
        visual = jnp.repeat(keep[:, c, :, 0], vlen, axis=1)
        keep_rows.append(jnp.concatenate([text, visual], axis=1)[:, :, None])

    kinds = jnp.transpose(qkv_weight, (0, 2, 1, 3))
    cross_weights = jnp.stack(
        [
            jnp.stack([kinds[0, 0], kinds[1, 1], kinds[1, 2]]),
            jnp.stack([kinds[1, 0], kinds[0, 1], kinds[0, 2]]),
        ]
    )
    self_weights = kinds[2:]
    weights = (cross_weights, self_weights)
    outs = (out_weight[:2], out_weight[2:])
    gains = [row_wise((norm_gain[2 * s], norm_gain[2 * s + 1])) for s in range(3)]
    shifts = [row_wise((norm_shift[2 * s], norm_shift[2 * s + 1])) for s in range(3)]

    now = [v.astype(F32) for v in join(text_blocks, visual_blocks)]
    cotangents = join(text_cotangent, visual_cotangent)
    inputs = [list(now), None, None]
    gathered = [[None] * CHUNKS for _ in range(3)]
    saved = [[None] * CHUNKS for _ in range(2)]
    gates = [None] * CHUNKS
    cots = [gather_start(cotangents[c]) for c in range(CHUNKS)]
    for s in range(2):
        started = []
        for c in range(CHUNKS):
            if s:
                now[c] = now[c] + scatter_end(ended[c], gates[-1])
                inputs[s][c] = now[c]
            started.append(gather_start(normalize(now[c], gains[s], shifts[s])))
        inputs[s + 1] = [None] * CHUNKS
        ended = []
        previous = None
        for c in range(CHUNKS):
            gate = cots[s][1] if c == CHUNKS - 1 else None
            gathered[s][c] = gather_end(started[c], previous, gate)
            parts, saved[s][c] = attend(
                gathered[s][c],
                weights[s],
                outs[s],
                keep_rows[c] if s == 0 else None,
                tlen,
                vlen,
                pages,
            )
            gates[c] = parts[0]
            ended.append(scatter_start(parts))
            previous = ended[c][3]
    grads_now = [v.astype(F32) for v in cotangents]
    scale_sums = [None] * 3
    shift_sums = [None] * 3

    def back(s, c, ended, *earlier):
        grad = scatter_end(ended, gates[-1], *earlier)
        delta, product = normalize_back(inputs[s][c], gains[s], grad)
        grads_now[c] = grads_now[c] + delta
        sums = [jnp.sum(v, axis=0) for v in (product[:trows], product[trows:])]
        shifts = [jnp.sum(v, axis=0) for v in (grad[:trows], grad[trows:])]
        sums, shifts = jnp.stack(sums), jnp.stack(shifts)
        scale_sums[s] = sums if scale_sums[s] is None else scale_sums[s] + sums
        shift_sums[s] = shifts if shift_sums[s] is None else shift_sums[s] + shifts

    started = []
    for c in range(CHUNKS):
        now[c] = now[c] + scatter_end(ended[c], gates[-1])
        inputs[2][c] = now[c]
        started.append(gather_start(normalize(now[c], gains[2], shifts[2])))
    partial, ended, outputs = [], [], []
    previous = None
    for c in range(CHUNKS):
        rows_all = gather_end(started[c], previous)
        cot = gather_end(cots[c])
        out, parts, grads = feed(rows_all, cot, up_weight, down_weight, trows)
        gates[c] = parts[0]
        partial.append(grads.astype(F32))
        ended.append(scatter_start(parts))
        previous = ended[c][3]
        outputs.append(out)
    rings = [None, None, Ring(sum(partial).astype(BF16), count)]
    for s in (1, 0):
        started = []
        for c in range(CHUNKS):
            back(s + 1, c, ended[c])
            started.append(gather_start(grads_now[c].astype(BF16)))
        partial, ended = [], []
        previous = None
        for c in range(CHUNKS):
            gate = None
            if s == 0:
                gate = rings[2].state()
                rings[2].hop()
            parts, grads = attend_back(
                gathered[s][c],
                gather_end(started[c], previous, gate),
                saved[s][c],
                weights[s],
                outs[s],
                keep_rows[c] if s == 0 else None,
                tlen,
                vlen,
                pages,
            )
            if c == 0:
                outputs[1 - s] = scatter_start(after(outputs[1 - s], parts[0]))
            gates[c] = parts[0]
            partial.append(grads.astype(F32))
            ended.append(scatter_start(parts))
            previous = ended[c][3]
        rings[s] = Ring(after(sum(partial).astype(BF16), rings[s + 1].mine), count)
    for c in range(CHUNKS):
        gate = rings[2].state()
        rings[2].hop()
        back(0, c, ended[c], gate)
        now[c] = now[c] + scatter_end(outputs[c])
    totals = [ring.total() for ring in rings]

    small = jnp.concatenate(scale_sums + shift_sums)
    for bit in (1, 2):
        small = small + swap(small, "mp", bit, 4)
    bit = 1
    while bit < count:
        small = small + swap(small, "dp", bit, count)
        bit *= 2

    text_output, visual_output = part(now)
    text_gradient, visual_gradient = part(grads_now)
    in_parts = [t[: 6 * width].reshape(2, 3, width, depth) for t in totals[:2]]
    cross = in_parts[0]
    cross = jnp.stack(
        [
            jnp.stack([cross[0, 0], cross[1, 1], cross[1, 2]]),
            jnp.stack([cross[1, 0], cross[0, 1], cross[0, 2]]),
        ]
    )
    in_grads = jnp.transpose(jnp.concatenate([cross, in_parts[1]]), (0, 3, 1, 2))
    out_grads = jnp.concatenate([t[6 * width :].reshape(2, width, depth) for t in totals[:2]])
    hid = up_weight.shape[2]
    up_grads = totals[2][: 2 * depth].reshape(2, depth, hid)
    down_grads = totals[2][2 * depth :].reshape(2, hid, depth)
    return (
        text_output,
        visual_output,
        text_gradient,
        visual_gradient,
        in_grads,
        out_grads,
        up_grads,
        down_grads,
        small[:6],
        small[6:],
    )


def solution(mesh):
    placed = (
        P(("dp", "mp"), None, None),
        P(("dp", "mp"), None, None),
        P("dp", None),
        P(None, None, None, "mp"),
        P(None, "mp", None),
        P(None, None, "mp"),
        P(None, "mp", None),
        P(),
        P(),
        P(("dp", "mp"), None, None),
        P(("dp", "mp"), None, None),
    )
    count = mesh.shape["dp"]

    def device(*arrays):
        return per_device(count, *arrays)

    return jax.shard_map(
        device,
        mesh=mesh,
        in_specs=placed,
        out_specs=(
            P(("dp", "mp"), None, None),
            P(("dp", "mp"), None, None),
            P(("dp", "mp"), None, None),
            P(("dp", "mp"), None, None),
            P(None, None, None, "mp"),
            P(None, "mp", None),
            P(None, None, "mp"),
            P(None, "mp", None),
            P(),
            P(),
        ),
        check_vma=False,
    )
```
